32 devices in a mesh: rep: 2 (over core), exp: 16 (over z, y, x).
Axes of the slice: x: 2, y: 2, z: 4, core: 2. Of those that a mesh axis runs over, the one named last changes fastest.
Arguments:
- attn_out: bfloat16 [4096, 2048], P(('rep', 'exp')), may hold values from -6 to 6
- resid: bfloat16 [4096, 1024], P(('rep', 'exp')), may hold values from -6 to 6
- out_grad: bfloat16 [4096, 1024], P(('rep', 'exp')), may hold values from -6 to 6
- gain: float32 [1024], replicated, may hold values from 0.5 to 1.5
- expert_ids: int32 [4096, 8], P(('rep', 'exp')), may hold values from 0 to 15, all different within a row; in each aligned block of 128 rows (0 to 127, 128 to 255, ...) at most 72 rows name the same one
- gate_vals: float32 [4096, 8], P(('rep', 'exp')), may hold values from 0.03 to 0.5
- w_gate: bfloat16 [16, 1024, 512], P('exp'), may hold values from -0.1875 to 0.1875
- w_up: bfloat16 [16, 1024, 512], P('exp'), may hold values from -0.1875 to 0.1875
- w_down: bfloat16 [16, 512, 1024], P('exp'), may hold values from -0.25 to 0.25
Outputs:
- d_resid: bfloat16 [4096, 1024], P(('rep', 'exp'))
- projection_grad: float32 [2048, 1024], P(('rep', 'exp'))
- gate_grad: float32 [16, 1024, 512], P('exp', None, 'rep')
- up_grad: float32 [16, 1024, 512], P('exp', None, 'rep')
- down_grad: float32 [16, 512, 1024], P('exp', None, 'rep')
The draws below stay inside these ranges and needn't reach their ends.
Inputs may be any that keep to these rules, and one draw needn't show every extreme that they name: `expert_ids`: each row names 8 different experts. Among the rows of one device no expert is named more than 72 times, a bound that some block reaches.
All inputs are finite; a program needn't handle non-finite values.
Results may differ from the reference program's by a relative error of at most 0.0095.
Values may be sent and summed in bfloat16 or wider, within the bound.
A program may use at most 128 MiB of HBM per device.

```python
import math
import jax
import jax.numpy as jnp
import numpy as np
from jax import lax

D = 1024
FF = 512
ATTN = 2048
TOP = 8
TOK_DEV = 128
EXPERTS = 16
CAP = 72
TOKENS = 4096
N_REP = 2
N_EXP = 16


def spiked(result, stream_key, source, target, blocks, factor):
    owner, partner = [(jnp.arange(result.shape[dim]) // (result.shape[dim] // blocks)).reshape([-1 if axis == dim else 1 for axis in range(result.ndim)]) for dim in (source, target)]
    chosen = jax.random.permutation(stream_key, blocks)[partner]
    strong = (owner == chosen) | (owner == (partner + blocks // 2) % blocks)
    return jnp.where(strong, factor * result, result)


def block_scale(key, shape, pieces, smallest, largest):
    level = 1.0
    for dim, parts in pieces:
        heights = jax.random.uniform(jax.random.fold_in(jax.random.fold_in(key, 6), dim), (parts,), jnp.float32, smallest / len(pieces), largest / len(pieces))
        level = level * jnp.repeat(jnp.exp(heights), shape[dim] // parts).reshape((-1,) + (1,) * (len(shape) - 1 - dim))
    return level


def assign_block(rng, own, number, rows, number_of, top, most, slope):
    sequence = jax.random.permutation(rng, number_of)
    packed, ordinary = portions_of(number_of, rows * top, most, slope, True), portions_of(number_of, rows * top, most, slope, False)
    places = jnp.arange(number_of)

    def named(sizes, turn):
        used = int((sizes > 0).sum())
        fixed = max(1, used // 4)
        passed = fixed + (places - fixed + turn * (used - fixed)) % max(1, number_of - fixed)
        return jnp.zeros((number_of,), jnp.int32).at[sequence[jnp.where(places < fixed, places, passed)]].set(jnp.asarray(sizes, jnp.int32))

    sizes = jnp.where(number % 4 == 0, named(packed, number // 4), named(ordinary, number - number // 4 - 1))
    mixed = jax.random.permutation(jax.random.fold_in(own, 3), number_of)
    source_of, taker = mixed[0:number_of // 2 * 2:2], mixed[1:number_of // 2 * 2:2]
    room = jnp.minimum(sizes[source_of] - 1, most - sizes[taker]) // 2
    room = jnp.where((source_of == sequence[0]) | (taker == sequence[0]) | (sizes[taker] == 0), 0, jnp.maximum(room, 0))
    passed = jax.random.randint(jax.random.fold_in(own, 4), (number_of // 2,), 0, 1 << 20) % (room + 1)
    sizes = sizes.at[source_of].add(-passed).at[taker].add(passed)
    labels = jnp.searchsorted(jnp.cumsum(sizes), jnp.arange(rows * top), side="right").astype(jnp.int32)
    grid = labels.reshape(top, rows).T
    grid = grid[jax.random.permutation(jax.random.fold_in(own, 1), rows)]
    turn = jax.random.randint(jax.random.fold_in(own, 2), (rows, 1), 0, top)
    return jnp.take_along_axis(grid, (jnp.arange(top)[None, :] + turn) % top, axis=1)


def portions_of(amount, total, limit, skew, full):
    weights = [(1 << 20) // math.isqrt(standing ** skew) + 1 for standing in range(1, amount + 1)]
    largest = limit if full else min(limit, max(-(-total // amount), total * weights[0] // sum(weights)))
    least = 1 if total - largest >= amount - 1 else 0
    given, spare = [largest] + [least] * (amount - 1), total - largest - least * (amount - 1)
    while spare > 0:
        free = [i for i in range(1, amount) if given[i] < largest] or [i for i in range(1, amount) if given[i] < limit]
        mass, left = sum([weights[i] for i in free]), spare
        for i in free:
            more = min(limit - given[i], max(1, left * weights[i] // mass), spare)
            given[i] = given[i] + more
            spare = spare - more
    return np.array(given)


def scatter_about(own_key, extent, deviation, limit, split=(), kind=jnp.bfloat16):
    result = deviation * jax.random.normal(own_key, extent, jnp.float32)
    if split:
        result = result * block_scale(own_key, extent, split, -0.22, 0.18)
    return jnp.clip(result, -limit, limit).astype(kind)


def bell_draw_with(rng, extent, scale, bound, shards, heavy, held_as=jnp.bfloat16):
    result = scale * jax.random.normal(rng, extent, jnp.float32)
    if shards:
        result = result * block_scale(rng, extent, shards, -0.22, 0.18)
    return jnp.clip(spiked(result, jax.random.fold_in(rng, 3), *heavy), -bound, bound).astype(held_as)


def setup_inputs(seed: int = 0) -> dict:
    arg_keys = jax.random.split(jax.random.key(seed), 10)
    attn_out = bell_draw_with(arg_keys[0], (TOKENS, ATTN), 1.0, 6.0, ((0, 32),), (0, 1, 32, 2.75))
    resid = scatter_about(arg_keys[1], (TOKENS, D), 1.0, 6.0, ((0, 32),))
    out_grad = scatter_about(arg_keys[2], (TOKENS, D), 1.0, 6.0, ((0, 32),))
    gain = jnp.clip(1.0 + 0.1 * jax.random.normal(arg_keys[3], (D,), jnp.float32), 0.5, 1.5)
    expert_ids_keys = jax.random.split(jax.random.fold_in(arg_keys[4], 1), TOKENS // TOK_DEV)
    expert_ids_turns = jax.random.permutation(jax.random.fold_in(arg_keys[4], 3), TOKENS // TOK_DEV)
    expert_ids = jax.vmap(lambda own, number: assign_block(jax.random.fold_in(arg_keys[4], 2), own, number, TOK_DEV, EXPERTS, TOP, CAP, 2))(expert_ids_keys, expert_ids_turns).reshape((TOKENS, TOP))
    gate_vals = jnp.clip(jnp.exp(math.log(0.5) - 2.8134107 * jax.random.uniform(arg_keys[5], (TOKENS, TOP), jnp.float32) ** block_scale(arg_keys[5], (TOKENS, TOP), ((0, 32),), -0.2, 0.2)), 0.03, 0.5)
    w_gate = scatter_about(arg_keys[6], (EXPERTS, D, FF), D ** -0.5, 0.1875, ((0, 16),))
    w_up = scatter_about(arg_keys[7], (EXPERTS, D, FF), D ** -0.5, 0.1875, ((0, 16),))
    w_down = scatter_about(arg_keys[8], (EXPERTS, FF, D), FF ** -0.5, 0.25, ((0, 16),))
    return dict(attn_out=attn_out, resid=resid, out_grad=out_grad, gain=gain, expert_ids=expert_ids, gate_vals=gate_vals, w_gate=w_gate, w_up=w_up, w_down=w_down)


epsilon = 1e-06

def slot_numbers(flat_ids, experts):
    onehot = (flat_ids[:, None] == jnp.arange(experts, dtype=jnp.int32)[None, :]).astype(jnp.int32)
    before = jnp.cumsum(onehot, axis=0) - onehot
    return lax.optimization_barrier(jnp.sum(before * onehot, axis=1)).astype(jnp.int32)

def silu_slope(pre):
    sigma = jax.nn.sigmoid(pre)
    return sigma * (1.0 + pre * (1.0 - sigma))

def expert_backward(rows_in, rows_grad, gate_matrix, up_matrix, down_matrix):
    pre_gate = jnp.dot(rows_in, gate_matrix, preferred_element_type=jnp.float32)
    pre_up = jnp.dot(rows_in, up_matrix, preferred_element_type=jnp.float32)
    active = jax.nn.silu(pre_gate)
    hidden = (active * pre_up).astype(jnp.bfloat16)
    d_hidden = jnp.dot(rows_grad, down_matrix.T, preferred_element_type=jnp.float32)
    down_part = jnp.dot(hidden.T, rows_grad, preferred_element_type=jnp.float32)
    d_gate = (d_hidden * pre_up * silu_slope(pre_gate)).astype(jnp.bfloat16)
    d_up = (d_hidden * active).astype(jnp.bfloat16)
    gate_part = jnp.dot(rows_in.T, d_gate, preferred_element_type=jnp.float32)
    up_part = jnp.dot(rows_in.T, d_up, preferred_element_type=jnp.float32)
    back = jnp.dot(d_gate, gate_matrix.T, preferred_element_type=jnp.float32)
    back = back + jnp.dot(d_up, up_matrix.T, preferred_element_type=jnp.float32)
    return (gate_part, up_part, down_part, back.astype(jnp.bfloat16))

def reference(attn_out, resid, out_grad, gain, expert_ids, gate_vals, w_gate, w_up, w_down):
    devices = N_REP * N_EXP
    per_device = TOK_DEV * TOP
    resid_f = resid.astype(jnp.float32)
    inv_rms = lax.rsqrt(lax.optimization_barrier(jnp.mean(resid_f * resid_f, axis=1, keepdims=True)) + epsilon)
    normed = resid_f * inv_rms
    gain_f = gain.astype(jnp.float32)[None, :]
    moe_in = (normed * gain_f).astype(jnp.bfloat16)
    device_ids = expert_ids.reshape(devices, per_device)
    slots = jax.vmap(lambda row_ids: slot_numbers(row_ids, EXPERTS))(device_ids)
    device_of = jnp.arange(devices, dtype=jnp.int32)[:, None]
    position = (device_of * CAP + slots).reshape(-1).astype(jnp.int32)
    table = jnp.full((EXPERTS, devices * CAP), -1, jnp.int32)
    table = table.at[expert_ids.reshape(-1), position].set(jnp.arange(TOKENS * TOP, dtype=jnp.int32))
    gate_flat = gate_vals.reshape(-1)

    def one_expert(total, inputs):
        index, gate_matrix, up_matrix, down_matrix = inputs
        valid = (index >= 0)[:, None]
        safe = jnp.maximum(index, 0).astype(jnp.int32)
        token = (safe // TOP).astype(jnp.int32)
        rows_in = jnp.where(valid, moe_in[token], jnp.zeros((), jnp.bfloat16))
        scaled = out_grad[token].astype(jnp.float32) * gate_flat[safe][:, None]
        rows_grad = jnp.where(valid, scaled, jnp.zeros((), jnp.float32)).astype(jnp.bfloat16)
        gate_part, up_part, down_part, back = expert_backward(rows_in, rows_grad, gate_matrix, up_matrix, down_matrix)
        added = jnp.where(valid, back.astype(jnp.float32), jnp.zeros((), jnp.float32))
        total = total.at[token].add(added)
        return (total, (gate_part, up_part, down_part))
    start = jnp.zeros((TOKENS, D), jnp.float32)
    d_moe, grads = lax.scan(one_expert, start, (table, w_gate, w_up, w_down))
    gate_grad, up_grad, down_grad = grads
    d_norm = d_moe * gain_f
    inner = lax.optimization_barrier(jnp.mean(d_norm * normed, axis=1, keepdims=True))
    d_resid = (out_grad.astype(jnp.float32) + inv_rms * (d_norm - normed * inner)).astype(jnp.bfloat16)
    projection_grad = jnp.dot(attn_out.T, d_resid, preferred_element_type=jnp.float32)
    return (d_resid, projection_grad, gate_grad, up_grad, down_grad)
```

```python
import functools

import jax
import jax.numpy as jnp
from jax import lax
from jax.experimental import pallas as pl
from jax.experimental.pallas import tpu as pltpu
from jax.sharding import PartitionSpec as P

epsilon = 1e-06
MESH = pl.DeviceIdType.MESH
NEAR_BY_LINE = (True, False, False)


def contract_rows(left, right):
    return lax.dot_general(
        left, right, (((0,), (0,)), ((), ())), preferred_element_type=jnp.float32
    )


def contract_last(left, right):
    return lax.dot_general(
        left, right, (((1,), (1,)), ((), ())), preferred_element_type=jnp.float32
    )


def grid_of(owners):
    inner = 2 if owners % 2 == 0 else 1
    middle = 2 if owners % 4 == 0 else 1
    return owners // (inner * middle), middle, inner


class Place:
    def __init__(self, owners):
        self.depth, self.middle, self.inner = grid_of(owners)
        assert self.middle == 2 and self.inner == 2
        self.rep = lax.axis_index("rep")
        me = lax.axis_index("exp")
        x = lax.rem(me, 2)
        y = lax.rem(me // 2, 2)
        self.z = me // 4
        self.me = me
        step_x, step_y = 1 - 2 * x, 2 - 4 * y
        turn = lax.rem(self.rep, 2)
        self.near = (1 - turn) * step_x + turn * step_y
        self.far = turn * step_x + (1 - turn) * step_y
        self.base = me - 4 * self.z

    def line(self, shift, k):
        return self.base + shift + 4 * lax.rem(self.z + k, self.depth)

    def device(self, owner):
        return (self.rep, owner)

    def greet(self, extra=()):
        barrier = pltpu.get_barrier_semaphore()
        partners = [self.device(self.line(0, k)) for k in range(1, self.depth)]
        partners += [self.device(self.me + self.near), self.device(self.me + self.far)]
        partners += list(extra)
        for partner in partners:
            pl.semaphore_signal(barrier, inc=1, device_id=partner, device_id_type=MESH)
        pl.semaphore_wait(barrier, len(partners))


def gather_kernel(owners, x_ref, out_ref, own_sem, send_sem, recv_sem):
    at = Place(owners)
    depth = at.depth
    at.greet()

    def copy(source, owner, slot, target):
        return pltpu.make_async_remote_copy(
            src_ref=source,
            dst_ref=out_ref.at[owner],
            send_sem=send_sem.at[slot],
            recv_sem=recv_sem.at[slot],
            device_id=at.device(target),
            device_id_type=MESH,
        )

    def arrived(owner, slot):
        copy(out_ref.at[owner], owner, slot, at.me).wait_recv()

    near, far = at.me + at.near, at.me + at.far
    line_slot = lambda k: k - 1
    near_slot = lambda k: depth - 1 + k
    far_slot = lambda k: 2 * depth - 1 + k
    turn_slot = lambda k: 3 * depth - 1 + k
    own = pltpu.make_async_copy(x_ref, out_ref.at[at.me], own_sem)
    own.start()
    sent = []

    def send(*what):
        one = copy(*what)
        one.start()
        sent.append(one)

    send(x_ref, at.me, near_slot(0), near)
    send(x_ref, at.me, far_slot(0), far)
    for k in range(1, depth):
        send(x_ref, at.me, line_slot(k), at.line(0, k))
    for k in range(depth):
        back = depth - k
        if k > 0:
            owner = at.line(0, back)
            arrived(owner, line_slot(k))
            send(out_ref.at[owner], owner, near_slot(k), near)
            send(out_ref.at[owner], owner, far_slot(k), far)
        owner = at.line(at.near, back)
        arrived(owner, near_slot(k))
        send(out_ref.at[owner], owner, turn_slot(k), far)
    for k in range(depth):
        arrived(at.line(at.far, depth - k), far_slot(k))
    for k in range(depth):
        arrived(at.line(at.near + at.far, depth - k), turn_slot(k))
    own.wait()
    for one in sent:
        one.wait_send()


def gather_owners(x, owners):
    depth = grid_of(owners)[0]
    copies = 4 * depth - 1
    return pl.pallas_call(
        functools.partial(gather_kernel, owners),
        out_shape=jax.ShapeDtypeStruct((owners,) + x.shape, x.dtype),
        in_specs=[pl.BlockSpec(memory_space=pltpu.VMEM)],
        out_specs=pl.BlockSpec(memory_space=pl.ANY),
        scratch_shapes=[
            pltpu.SemaphoreType.DMA,
            pltpu.SemaphoreType.DMA((copies,)),
            pltpu.SemaphoreType.DMA((copies,)),
        ],
        compiler_params=pltpu.CompilerParams(collective_id=0, has_side_effects=True),
        name="gather_owners",
    )(x)


def scatter_kernel(
    owners, replicas, p_ref, out_ref, rep_in, far_in, near_in, line_in, work, *sems
):
    at = Place(owners)
    depth = at.depth
    (rep_send, rep_recv, far_send, far_recv, near_send, near_recv, line_send, line_recv) = sems
    others = [(lax.rem(at.rep + j, replicas), at.me) for j in range(1, replicas)]
    at.greet(others)
    sent = []

    def copy(source, target, send_sem, recv_sem, device):
        return pltpu.make_async_remote_copy(
            src_ref=source,
            dst_ref=target,
            send_sem=send_sem,
            recv_sem=recv_sem,
            device_id=device,
            device_id_type=MESH,
        )

    lines = [at.near + at.far, at.far, at.near, 0]
    order = [k for k in range(1, depth)] + [0]
    near, far = at.device(at.me + at.near), at.device(at.me + at.far)

    def rep_copy(j, owner):
        return copy(
            p_ref.at[lax.rem(at.rep + j, replicas), owner],
            rep_in.at[j - 1, owner],
            rep_send.at[j - 1, owner],
            rep_recv.at[j - 1, owner],
            (lax.rem(at.rep + j, replicas), at.me),
        )

    for k in range(depth):
        for line in range(4):
            for j in range(1, replicas):
                one = rep_copy(j, at.line(lines[line], order[k]))
                one.start()
                sent.append(one)

    def own(line, k):
        owner = at.line(lines[line], order[k])
        total = p_ref[at.rep if replicas > 1 else 0, owner].astype(jnp.float32)
        for j in range(1, replicas):
            rep_copy(j, owner).wait_recv()
            total = total + rep_in[j - 1, owner].astype(jnp.float32)
        return total

    def far_copy(number):
        return copy(
            work.at[number], far_in.at[number], far_send.at[number], far_recv.at[number], far
        )

    for k in range(depth):
        for line in range(2):
            number = line * depth + k
            work[number] = own(line, k).astype(work.dtype)
            one = far_copy(number)
            one.start()
            sent.append(one)

    def near_copy(k):
        return copy(
            work.at[2 * depth + k], near_in.at[k], near_send.at[k], near_recv.at[k], near
        )

    def near_step(k):
        total = own(2, k)
        far_copy(k).wait_recv()
        work[2 * depth + k] = (total + far_in[k].astype(jnp.float32)).astype(work.dtype)
        one = near_copy(k)
        one.start()
        sent.append(one)

    def line_step(k):
        number = 3 * depth + k
        total = own(3, k)
        far_copy(depth + k).wait_recv()
        near_copy(k).wait_recv()
        total = total + far_in[depth + k].astype(jnp.float32) + near_in[k].astype(jnp.float32)
        if order[k] > 0:
            work[number] = total.astype(work.dtype)
            one = copy(
                work.at[number],
                line_in.at[k],
                line_send.at[k],
                line_recv.at[k],
                at.device(at.line(0, order[k])),
            )
            one.start()
            sent.append(one)
        return total

    for k in range(depth):
        near_step(k)
        if k > 0:
            line_step(k - 1)
    total = line_step(depth - 1)
    for k in range(depth - 1):
        copy(work.at[0], line_in.at[k], line_send.at[k], line_recv.at[k], near).wait_recv()
        total = total + line_in[k].astype(jnp.float32)
    out_ref[...] = total
    for one in sent:
        one.wait_send()


def product_kernel(owners, replicas, left_ref, right_ref, out_ref, p_ref, *rest):
    rows = p_ref.shape[2]
    tile = 2 * rows
    for i in range(replicas * owners // 2):
        part = contract_rows(left_ref[:, i * tile : (i + 1) * tile], right_ref[...])
        part = part.astype(p_ref.dtype)
        for half in range(2):
            p_ref[(2 * i + half) // owners, (2 * i + half) % owners] = part[
                half * rows : (half + 1) * rows
            ]
    scatter_kernel(owners, replicas, p_ref, out_ref, *rest)


def scatter_owners(shape, number, *operands):
    replicas, owners, rows, columns = shape
    kind = jnp.bfloat16
    fused = len(operands) == 2
    p = pltpu.VMEM(shape, kind)
    depth = grid_of(owners)[0]
    dma = pltpu.SemaphoreType.DMA
    many = max(1, replicas - 1)
    rep_slots = owners if replicas > 1 else 1
    return pl.pallas_call(
        functools.partial(product_kernel if fused else scatter_kernel, owners, replicas),
        out_shape=jax.ShapeDtypeStruct((rows, columns), jnp.float32),
        in_specs=[pl.BlockSpec(memory_space=pltpu.VMEM)] * len(operands),
        out_specs=pl.BlockSpec(memory_space=pltpu.VMEM),
        scratch_shapes=[p] * fused
        + [
            pltpu.VMEM((many, rep_slots, rows, columns), kind),
            pltpu.VMEM((2 * depth, rows, columns), kind),
            pltpu.VMEM((depth, rows, columns), kind),
            pltpu.VMEM((depth, rows, columns), kind),
            pltpu.VMEM((4 * depth, rows, columns), kind),
            dma((many, rep_slots)),
            dma((many, rep_slots)),
            dma((2 * depth,)),
            dma((2 * depth,)),
            dma((depth,)),
            dma((depth,)),
            dma((depth,)),
            dma((depth,)),
        ],
        compiler_params=pltpu.CompilerParams(
            collective_id=number, has_side_effects=True, vmem_limit_bytes=60 * 2**20
        ),
        name="scatter_owners",
    )(*operands)


def steps_of(depth, z):
    side = jnp.minimum(z, depth - 1 - z)
    planes = [z]
    for k in range(1, depth):
        turn = z - (k + 1) // 2 if k % 2 else z + k // 2
        rest = jnp.where(z > depth - 1 - z, z - (k - side), z + (k - side))
        planes.append(jnp.where(k <= 2 * side, turn, rest))
    return planes


def expert_kernel(
    owners, replicas, cap, near_by_line, resid_ref, grad_ref, gain_ref, ids_ref, vals_ref,
    gate_hbm, up_hbm, down_hbm, out_ref, gate_out, up_out, down_out,
    wide_ref, deep_ref, got_x, got_g, got_t, pick_ref, all_x, all_g, all_d, all_h,
    leaf_x, leaf_g, ret, leaf_back, root_sum, near_work, near_in, line_work, line_in,
    first_ref, second_ref, gate_away, up_away, down_away, gate_came, up_came, down_came,
    load_sem, own_send, hop_send, line_recv, side_send, side_recv, leaf_send, leaf_recv,
    back_send, back_recv, near_send, near_recv, home_send, home_recv, rep_send, rep_recv,
):
    at = Place(owners)
    depth, z = at.depth, at.z
    rows, feature = resid_ref.shape
    hidden = deep_ref.shape[0]
    pair = 2 * cap
    others = [(lax.rem(at.rep + j, replicas), at.me) for j in range(1, replicas)]
    planes = steps_of(depth, z)
    wide = lambda block: block.astype(jnp.float32)
    near, far = at.me + at.near, at.me + at.far
    owner_at = lambda plane: at.base + 4 * plane

    loads = [
        pltpu.make_async_copy(gate_hbm, wide_ref.at[:, pl.ds(0, hidden)], load_sem.at[0]),
        pltpu.make_async_copy(up_hbm, wide_ref.at[:, pl.ds(hidden, hidden)], load_sem.at[1]),
        pltpu.make_async_copy(down_hbm, deep_ref, load_sem.at[2]),
    ]
    for one in loads:
        one.start()

    resid = wide(resid_ref[...])
    inv_rms = lax.rsqrt(jnp.mean(resid * resid, axis=1, keepdims=True) + epsilon)
    normed = resid * inv_rms
    got_x[z, pl.ds(0, rows)] = (normed * gain_ref[...]).astype(jnp.bfloat16)
    got_g[z, pl.ds(0, rows)] = grad_ref[...]
    number = lax.broadcasted_iota(jnp.int32, (owners, rows), 0)
    table = jnp.zeros((owners, rows), jnp.float32)
    for j in range(ids_ref.shape[0]):
        table = table + jnp.where(ids_ref[j : j + 1, :] == number, vals_ref[j : j + 1, :], 0.0)
    got_t[z, pl.ds(0, owners)] = table

    at.greet(others)
    sent = []

    def copy(source, target, send, recv, owner):
        return pltpu.make_async_remote_copy(
            src_ref=source,
            dst_ref=target,
            send_sem=send,
            recv_sem=recv,
            device_id=at.device(owner),
            device_id_type=MESH,
        )

    def start(one):
        one.start()
        sent.append((None, one))

    def start_if(ok, one):
        @pl.when(ok)
        def _():
            one.start()

        sent.append((ok, one))

    def piece(name, role, plane):
        if name == 2:
            return got_t.at[plane, pl.ds(role * owners, owners)]
        return (got_x, got_g)[name].at[plane, pl.ds(role * rows, rows)]

    def own_hops(role, name):
        for way in range(2):
            target = z + 1 - 2 * way
            block = piece(name, role, z)
            start_if(
                (target >= 0) & (target < depth),
                copy(
                    block, block, own_send.at[role, name, way], line_recv.at[role, name, z],
                    owner_at(target),
                ),
            )

    def hop(role, name, k):
        plane = planes[k]
        block = piece(name, role, plane)
        target = jnp.where(plane < z, z + 1, z - 1)
        one = copy(
            block, block, hop_send.at[role, name, k], line_recv.at[role, name, plane],
            owner_at(target),
        )
        one.wait_recv()
        start_if((target >= 0) & (target < depth), one)

    def side(name, k):
        return copy(
            piece(name, 0, planes[k]), piece(name, 1, planes[k]),
            side_send.at[name, k], side_recv.at[name, k], near,
        )

    by_line = lambda name, k: k > 0 and near_by_line[name]

    def relay(k, names):
        for name in names:
            if k == 0:
                own_hops(0, name)
            else:
                hop(0, name, k)
            if not by_line(name, k):
                start(side(name, k))

    def near_ready(k, names):
        for name in names:
            if by_line(name, k):
                hop(1, name, k)
            else:
                side(name, k).wait_recv()
                if k == 0 and near_by_line[name]:
                    own_hops(1, name)

    def leaf(name, k):
        target = (all_x, all_g)[name].at[pl.ds((2 * k + 1) * pair, pair)]
        source = (leaf_x, leaf_g)[name].at[k]
        return copy(source, target, leaf_send.at[name, k], leaf_recv.at[name, k], far)

    def select(k):
        plane = planes[k]
        near_ready(k, (2,))
        gates = got_t[plane]
        hit = gates > 0.0
        lower = lax.broadcasted_iota(jnp.int32, (rows, rows), 0)
        upper = lax.broadcasted_iota(jnp.int32, (rows, rows), 1)
        ramp = jnp.where(lower <= upper, 1.0, 0.0).astype(jnp.bfloat16)
        place = jnp.dot(
            jnp.where(hit, 1.0, 0.0).astype(jnp.bfloat16), ramp, preferred_element_type=jnp.float32
        )
        place = jnp.where(hit, place, 0.0)
        line = lax.broadcasted_iota(jnp.int32, gates.shape, 0)
        order = (lax.broadcasted_iota(jnp.int32, (cap, rows), 0) + 1).astype(jnp.float32)
        empty = jnp.zeros((cap, rows), jnp.float32)
        picks, weights = [], []
        for expert in (at.me, far):
            for role in range(2):
                mine = line == expert + role * owners
                spot = jnp.sum(jnp.where(mine, place, 0.0), axis=0, keepdims=True)
                value = jnp.sum(jnp.where(mine, gates, 0.0), axis=0, keepdims=True)
                one_hot = jnp.where(order == spot, 1.0, 0.0)
                weights.append(jnp.sum(one_hot * value, axis=1, keepdims=True))
                picks.append(
                    jnp.concatenate([one_hot, empty] if role == 0 else [empty, one_hot], axis=1)
                )
        pick = jnp.concatenate(picks, axis=0).astype(jnp.bfloat16)
        weight = jnp.concatenate(weights, axis=0)
        pick_ref[k] = pick
        low = 2 * k * pair
        near_ready(k, (0,))
        chosen = jnp.dot(pick, got_x[plane], preferred_element_type=jnp.float32)
        chosen = chosen.astype(jnp.bfloat16)
        leaf_x[k] = chosen[pair:]
        start(leaf(0, k))
        all_x[low : low + pair] = chosen[:pair]
        near_ready(k, (1,))
        chosen = jnp.dot(pick, got_g[plane], preferred_element_type=jnp.float32) * weight
        chosen = chosen.astype(jnp.bfloat16)
        leaf_g[k] = chosen[pair:]
        start(leaf(1, k))
        all_g[low : low + pair] = chosen[:pair]

    def compute(k, half):
        low = (2 * k + half) * pair
        rows_in, rows_grad = all_x[low : low + pair], all_g[low : low + pair]
        matrix = wide_ref[...]
        pre = jnp.dot(rows_in, matrix, preferred_element_type=jnp.float32)
        d_hidden = contract_last(rows_grad, deep_ref[...])
        pre_gate, pre_up = pre[:, :hidden], pre[:, hidden:]
        sigma = jax.nn.sigmoid(pre_gate)
        active = pre_gate * sigma
        all_h[low : low + pair] = (active * pre_up).astype(jnp.bfloat16)
        d_gate = (d_hidden * pre_up * (sigma * (1.0 + pre_gate * (1.0 - sigma)))).astype(
            jnp.bfloat16
        )
        d_up = (d_hidden * active).astype(jnp.bfloat16)
        all_d[low : low + pair, :hidden] = d_gate
        all_d[low : low + pair, hidden:] = d_up
        back = contract_last(jnp.concatenate([d_gate, d_up], axis=1), matrix).astype(jnp.bfloat16)
        if half == 0:
            ret[k, :pair] = back
        else:
            leaf_back[k] = back
            start(back_copy(k))

    def back_copy(k):
        return copy(
            leaf_back.at[k], ret.at[k, pl.ds(pair, pair)], back_send.at[k], back_recv.at[k], far
        )

    def near_copy(k):
        return copy(near_work.at[k], near_in.at[k], near_send.at[k], near_recv.at[k], near)

    def home_copy(k, plane, slot):
        return copy(
            line_work.at[k], line_in.at[slot], home_send.at[k], home_recv.at[slot], owner_at(plane)
        )

    def leaf_step(k):
        leaf(0, k).wait_recv()
        leaf(1, k).wait_recv()
        compute(k, 1)

    def near_step(k):
        back_copy(k).wait_recv()
        total = contract_rows(pick_ref[k], ret[k])
        near_work[k] = total[rows:].astype(jnp.bfloat16)
        start(near_copy(k))
        root_sum[k] = total[:rows]

    def root_step(k):
        near_copy(k).wait_recv()
        total = root_sum[k] + wide(near_in[k])
        if k == 0:
            root_sum[k] = total
        else:
            line_work[k] = total.astype(jnp.bfloat16)
            start(home_copy(k, planes[k], z))

    def weights(first, last):
        low, high = 2 * first * pair, 2 * last * pair
        wide_part = contract_rows(all_x[low:high], all_d[low:high])
        deep_part = contract_rows(all_h[low:high], all_g[low:high])
        if first == 0:
            first_ref[...] = wide_part
            second_ref[...] = deep_part
        else:
            first_ref[...] += wide_part
            second_ref[...] += deep_part

    relay(0, (2, 0, 1))
    select(0)
    for one in loads:
        one.wait()
    for k in range(depth):
        if k + 1 < depth:
            relay(k + 1, (2, 0))
        compute(k, 0)
        if k + 1 < depth:
            relay(k + 1, (1,))
        if k > 0:
            near_step(k - 1)
        leaf_step(k)
        if k + 1 < depth:
            select(k + 1)
        if k > 0:
            root_step(k - 1)
        if k == depth // 2:
            weights(0, depth // 2)
    weights(depth // 2, depth)

    share, deep_share = hidden // replicas, feature // replicas
    trades = (
        (first_ref, 0, share, gate_away, gate_came, gate_out),
        (first_ref, hidden, share, up_away, up_came, up_out),
        (second_ref, 0, deep_share, down_away, down_came, down_out),
    )

    def part_of(i, member):
        ref, low, size = trades[i][:3]
        return ref[:, pl.ds(pl.multiple_of(low + member * size, 128), size)]

    def trade_copy(i, j):
        return pltpu.make_async_remote_copy(
            src_ref=trades[i][3].at[j - 1],
            dst_ref=trades[i][4].at[j - 1],
            send_sem=rep_send.at[i, j - 1],
            recv_sem=rep_recv.at[i, j - 1],
            device_id=others[j - 1],
            device_id_type=MESH,
        )

    for j in range(1, replicas):
        for i in range(3):
            trades[i][3][j - 1] = part_of(i, lax.rem(at.rep + j, replicas)).astype(jnp.bfloat16)
            start(trade_copy(i, j))
    near_step(depth - 1)
    for i in range(3):
        total = part_of(i, at.rep)
        for j in range(1, replicas):
            trade_copy(i, j).wait_recv()
            total = total + wide(trades[i][4][j - 1])
        trades[i][5][...] = total
    root_step(depth - 1)
    d_moe = root_sum[0]
    for k in range(1, depth):
        home_copy(k, z, planes[k]).wait_recv()
        d_moe = d_moe + wide(line_in[planes[k]])
    d_norm = d_moe * gain_ref[...]
    resid = wide(resid_ref[...])
    inv_rms = lax.rsqrt(jnp.mean(resid * resid, axis=1, keepdims=True) + epsilon)
    normed = resid * inv_rms
    inner = jnp.mean(d_norm * normed, axis=1, keepdims=True)
    out_ref[...] = (wide(grad_ref[...]) + inv_rms * (d_norm - normed * inner)).astype(jnp.bfloat16)
    for ok, one in sent:
        if ok is None:
            one.wait_send()
        else:
            pl.when(ok)(one.wait_send)


def expert_on_owners(
    resid, out_grad, gain, ids, vals, gate_matrix, up_matrix, down_matrix, cap, owners, replicas
):
    depth = grid_of(owners)[0]
    rows, feature = resid.shape
    hidden = gate_matrix.shape[1]
    dma = pltpu.SemaphoreType.DMA
    pair = 2 * cap
    vmem = pl.BlockSpec(memory_space=pltpu.VMEM)
    hbm = pl.BlockSpec(memory_space=pl.ANY)
    low = lambda *shape: pltpu.VMEM(shape, jnp.bfloat16)
    high = lambda *shape: pltpu.VMEM(shape, jnp.float32)
    many = max(1, replicas - 1)
    wide = lambda *shape: jax.ShapeDtypeStruct(shape, jnp.float32)
    shares = [
        (feature, hidden // replicas),
        (feature, hidden // replicas),
        (hidden, feature // replicas),
    ]
    return pl.pallas_call(
        functools.partial(expert_kernel, owners, replicas, cap, NEAR_BY_LINE),
        out_shape=(jax.ShapeDtypeStruct((rows, feature), jnp.bfloat16),)
        + tuple(wide(*shape) for shape in shares),
        in_specs=[vmem] * 5 + [hbm] * 3,
        out_specs=(vmem,) * 4,
        scratch_shapes=[
            low(feature, 2 * hidden),
            low(hidden, feature),
            low(depth, 2 * rows, feature),
            low(depth, 2 * rows, feature),
            high(depth, 2 * owners, rows),
            low(depth, 2 * pair, 2 * rows),
            low(depth * 2 * pair, feature),
            low(depth * 2 * pair, feature),
            low(depth * 2 * pair, 2 * hidden),
            low(depth * 2 * pair, hidden),
            low(depth, pair, feature),
            low(depth, pair, feature),
            low(depth, 2 * pair, feature),
            low(depth, pair, feature),
            high(depth, rows, feature),
            low(depth, rows, feature),
            low(depth, rows, feature),
            low(depth, rows, feature),
            low(depth, rows, feature),
            high(feature, 2 * hidden),
            high(hidden, feature),
            *(low(many, *shape) for shape in shares),
            *(low(many, *shape) for shape in shares),
            dma((3,)),
            dma((2, 3, 2)),
            dma((2, 3, depth)),
            dma((2, 3, depth)),
            dma((3, depth)),
            dma((3, depth)),
            dma((2, depth)),
            dma((2, depth)),
            dma((depth,)),
            dma((depth,)),
            dma((depth,)),
            dma((depth,)),
            dma((depth,)),
            dma((depth,)),
            dma((3, many)),
            dma((3, many)),
        ],
        compiler_params=pltpu.CompilerParams(
            collective_id=3, has_side_effects=True, vmem_limit_bytes=60 * 2**20
        ),
        name="expert_on_owners",
    )(resid, out_grad, gain, ids, vals, gate_matrix, up_matrix, down_matrix)


def share_replicas(part, replicas):
    member = lax.axis_index("rep")
    share = part.shape[1] // replicas
    total = lax.dynamic_slice_in_dim(part, member * share, share, 1)
    low = part.astype(jnp.bfloat16)
    for j in range(1, replicas):
        away = lax.dynamic_slice_in_dim(low, lax.rem(member + j, replicas) * share, share, 1)
        came = lax.ppermute(away, "rep", [(i, (i + j) % replicas) for i in range(replicas)])
        total = total + came.astype(jnp.float32)
    return total


def body(attn_out, resid, out_grad, gain, expert_ids, gate_vals, w_gate, w_up, w_down):
    owners = lax.axis_size("exp")
    replicas = lax.axis_size("rep")
    token_rows, top = expert_ids.shape
    feature = resid.shape[1]
    gain_f = gain[None, :]
    gate_matrix, up_matrix, down_matrix = w_gate[0], w_up[0], w_down[0]
    cap = 9 * token_rows * top // (8 * owners)
    held = owners * token_rows * 4 * feature * 2
    if held <= 32 * 2**20:
        d_resid, gate_out, up_out, down_out = expert_on_owners(
            resid, out_grad, gain_f, expert_ids.T, gate_vals.T, gate_matrix, up_matrix,
            down_matrix, cap, owners, replicas
        )
    else:
        d_resid, gate_out, up_out, down_out = experts_by_gather(
            resid, out_grad, gain_f, expert_ids, gate_vals, gate_matrix, up_matrix, down_matrix
        )
    rows = attn_out.shape[1] // (owners * replicas)
    shape = (replicas, owners, rows, feature)
    if rows % 64 == 0:
        projection_grad = scatter_owners(shape, 2, attn_out, d_resid)
    else:
        parts = contract_rows(attn_out, d_resid).astype(jnp.bfloat16)
        projection_grad = scatter_owners(shape, 2, parts.reshape(shape))
    return (d_resid, projection_grad, gate_out[None], up_out[None], down_out[None])


def experts_by_gather(
    resid, out_grad, gain_f, expert_ids, gate_vals, gate_matrix, up_matrix, down_matrix
):
    owners = lax.axis_size("exp")
    replicas = lax.axis_size("rep")
    token_rows = expert_ids.shape[0]
    feature = resid.shape[1]
    resid_f = resid.astype(jnp.float32)
    inv_rms = lax.rsqrt(jnp.mean(resid_f * resid_f, axis=1, keepdims=True) + epsilon)
    normed = resid_f * inv_rms
    moe_in = (normed * gain_f).astype(jnp.bfloat16)
    hit = expert_ids[:, :, None] == jnp.arange(owners, dtype=jnp.int32)[None, None, :]
    gates = jnp.sum(jnp.where(hit, gate_vals[:, :, None], 0.0), axis=1)
    high = gates.astype(jnp.bfloat16)
    low = (gates - high.astype(jnp.float32)).astype(jnp.bfloat16)
    spare = -(2 * owners) % 128
    sent = jnp.concatenate(
        [moe_in, out_grad, high, low, jnp.zeros((token_rows, spare), jnp.bfloat16)], axis=1
    )
    got = gather_owners(sent, owners).reshape(owners * token_rows, sent.shape[1])
    rows_in = got[:, :feature]
    expert = lax.axis_index("exp")
    pick = lambda start: lax.dynamic_slice_in_dim(
        got, start + expert, 1, 1
    ).astype(jnp.float32)
    gate = pick(2 * feature) + pick(2 * feature + owners)
    rows_grad = (got[:, feature : 2 * feature].astype(jnp.float32) * gate).astype(jnp.bfloat16)
    pre_gate = jnp.dot(rows_in, gate_matrix, preferred_element_type=jnp.float32)
    pre_up = jnp.dot(rows_in, up_matrix, preferred_element_type=jnp.float32)
    sigma = jax.nn.sigmoid(pre_gate)
    active = pre_gate * sigma
    hidden = (active * pre_up).astype(jnp.bfloat16)
    d_hidden = contract_last(rows_grad, down_matrix)
    d_gate = (d_hidden * pre_up * (sigma * (1.0 + pre_gate * (1.0 - sigma)))).astype(jnp.bfloat16)
    d_up = (d_hidden * active).astype(jnp.bfloat16)
    back = contract_last(d_gate, gate_matrix) + contract_last(d_up, up_matrix)
    d_moe = scatter_owners(
        (1, owners, token_rows, feature),
        1,
        back.astype(jnp.bfloat16).reshape(1, owners, token_rows, feature),
    )
    gate_part, up_part = contract_rows(rows_in, d_gate), contract_rows(rows_in, d_up)
    down_part = contract_rows(hidden, rows_grad)
    gate_out = share_replicas(gate_part, replicas)
    up_out = share_replicas(up_part, replicas)
    down_out = share_replicas(down_part, replicas)
    d_norm = d_moe * gain_f
    inner = jnp.mean(d_norm * normed, axis=1, keepdims=True)
    d_resid = (out_grad.astype(jnp.float32) + inv_rms * (d_norm - normed * inner)).astype(
        jnp.bfloat16
    )
    return d_resid, gate_out, up_out, down_out


def solution(mesh):
    in_specs = (
        P(("rep", "exp"), None),
        P(("rep", "exp"), None),
        P(("rep", "exp"), None),
        P(),
        P(("rep", "exp"), None),
        P(("rep", "exp"), None),
        P("exp", None, None),
        P("exp", None, None),
        P("exp", None, None),
    )
    out_specs = (
        P(("rep", "exp"), None),
        P(("rep", "exp"), None),
        P("exp", None, "rep"),
        P("exp", None, "rep"),
        P("exp", None, "rep"),
    )
    return jax.shard_map(body, mesh=mesh, in_specs=in_specs, out_specs=out_specs, check_vma=False)
```
